32 devices in a mesh: row: 4 (over z), col: 4 (over x, core), grp: 2 (over y).
Axes of the slice: x: 2, y: 2, z: 4, core: 2. Of those that a mesh axis runs over, the one named last changes fastest.
Arguments:
- matrix: float32 [16384, 16384], P('row', ('col', 'grp')), may hold values from -8 to 8, as said below
- basis_rows: float32 [4096, 16384], P(('col', 'grp'), 'row'), may hold values from -6 to 6
- reflectors: float32 [16384, 512], P('row'), may hold values from -0.125 to 0.125
- tfactor: float32 [512, 512], replicated, may hold values from -0.25 to 2, as said below
Outputs:
- new_matrix: float32 [16384, 16384], P('row', ('col', 'grp'))
- new_basis: float32 [4096, 16384], P(('col', 'grp'), 'row')
The draws below stay inside these ranges and needn't reach their ends.
Inputs may be any that keep to these rules, and one draw needn't show every extreme that they name: The matrix A that it represents is symmetric. `tfactor`: upper triangular: zero below the diagonal, diagonal between 1 and 2.
All inputs are finite; a program needn't handle non-finite values.
Results may differ from the reference program's by a relative error of at most 0.000073.
Values sent between devices are 32-bit elements; how exact they have to be, the bound alone decides.
A program may use at most 192 MiB of HBM per device.

```python
import jax
import jax.numpy as jnp
from jax import lax

M = 16384
NB = 512
ROWBLK = 4096
COLBLK = 2048
SLICE = 512
QROWS = 4096


def draw_matrix(key, part):
    first_key = jax.random.fold_in(key, 11)
    normal = jax.random.normal(first_key, (M, M), jnp.float32)
    symmetric = (normal + normal.T) * 0.70710678
    symmetric = jnp.clip(symmetric, -8.0, 8.0)
    nrow = M // ROWBLK
    ncol = M // COLBLK
    return symmetric.reshape(M, nrow, ncol, SLICE).transpose(0, 2, 1, 3).reshape(M, M)


def draw_tfactor(key, part):
    first_key = jax.random.fold_in(key, 21)
    second_key = jax.random.fold_in(key, 22)
    above = jnp.clip(jax.random.normal(first_key, (NB, NB), jnp.float32) * NB ** (-0.5), -0.25, 0.25)
    diag = jax.random.uniform(second_key, (NB,), jnp.float32, 1.0, 2.0)
    return jnp.triu(above, 1) + jnp.diag(diag)


def shard_levels(own_key, extent, shards, least, top_value):
    level, own = 1.0, jax.random.fold_in(own_key, 6)
    for dim, shards_of in shards:
        heights = jnp.exp(jax.random.uniform(jax.random.fold_in(own, dim), (shards_of,), jnp.float32, least / len(shards), top_value / len(shards)))
        level = level * jnp.repeat(heights, extent[dim] // shards_of).reshape([-1 if axis == dim else 1 for axis in range(len(extent))])
    return level


def gaussian(own_key, dims, deviation, most, pieces=(), held_as=jnp.bfloat16):
    loudness = shard_levels(own_key, dims, pieces, -0.22, 0.18) if pieces else 1.0
    array = jax.random.normal(own_key, dims, jnp.float32) * deviation * loudness
    return jnp.minimum(jnp.maximum(array, -most), most).astype(held_as)


def setup_inputs(seed: int = 0) -> dict:
    splits = jax.random.split(jax.random.key(seed), 5)
    return {
        "matrix": draw_matrix(jax.random.fold_in(splits[4], 71), 0),
        "basis_rows": gaussian(splits[1], (QROWS, M), 1.0, 6.0, ((0, 8), (1, 4)), jnp.float32),
        "reflectors": gaussian(splits[2], (M, NB), (4 * NB) ** -0.5, 0.125, ((0, 4),), jnp.float32),
        "tfactor": draw_tfactor(jax.random.fold_in(splits[4], 71), 0),
    }


def to_global(stored):
    nrow = M // ROWBLK
    ncol = M // COLBLK
    return stored.reshape(M, ncol, nrow, SLICE).transpose(0, 2, 1, 3).reshape(M, M)


def to_stored(full):
    nrow = M // ROWBLK
    ncol = M // COLBLK
    return full.reshape(M, nrow, ncol, SLICE).transpose(0, 2, 1, 3).reshape(M, M)


def reference(matrix, basis_rows, reflectors, tfactor):
    highest = lax.Precision.HIGHEST
    full = to_global(matrix)
    applied = jnp.dot(full, reflectors, precision=highest, preferred_element_type=jnp.float32)
    wide = jnp.dot(applied, tfactor, precision=highest, preferred_element_type=jnp.float32)
    cross = jnp.dot(reflectors.T, wide, precision=highest, preferred_element_type=jnp.float32)
    inner = jnp.dot(tfactor.T, cross, precision=highest, preferred_element_type=jnp.float32)
    zeta = wide - 0.5 * jnp.dot(reflectors, inner, precision=highest, preferred_element_type=jnp.float32)
    updated = full - jnp.dot(reflectors, zeta.T, precision=highest, preferred_element_type=jnp.float32)
    updated = updated - jnp.dot(zeta, reflectors.T, precision=highest, preferred_element_type=jnp.float32)
    q_proj = jnp.dot(basis_rows, reflectors, precision=highest, preferred_element_type=jnp.float32)
    q_fact = jnp.dot(q_proj, tfactor, precision=highest, preferred_element_type=jnp.float32)
    new_basis = basis_rows - jnp.dot(q_fact, reflectors.T, precision=highest, preferred_element_type=jnp.float32)
    return to_stored(updated), new_basis
```

```python
import jax
import jax.numpy as jnp
from jax import lax
from jax.experimental import pallas as pl
from jax.experimental.pallas import tpu as pltpu
from jax.sharding import PartitionSpec as P


def halves(x):
    high = x.astype(jnp.bfloat16)
    return high, (x - high.astype(jnp.float32)).astype(jnp.bfloat16)


def apply_kernel(index_ref, a_ref, v_ref, *rest):
    out_ref = rest[-1]
    a_high, a_low = halves(a_ref[...])
    v_high, v_low = halves(v_ref[...])
    product = jnp.dot(
        jnp.concatenate([a_high, a_low, a_high], axis=1),
        jnp.concatenate([v_high, v_high, v_low], axis=0),
        preferred_element_type=jnp.float32,
    )
    out_ref[...] = product if len(rest) == 1 else rest[0][...] + product


def apply_chunk(matrix, chunk, total, index):
    rows, (depth, wide) = matrix.shape[0], chunk.shape
    tile = min(512, rows)
    specs = [
        pl.BlockSpec((tile, depth), lambda i, c: (i, c[0])),
        pl.BlockSpec((depth, wide), lambda i, c: (0, 0)),
    ]
    args = [matrix, chunk]
    if total is not None:
        specs.append(pl.BlockSpec((tile, wide), lambda i, c: (i, 0)))
        args.append(total)
    return pl.pallas_call(
        apply_kernel,
        out_shape=jax.ShapeDtypeStruct((rows, wide), jnp.float32),
        grid_spec=pltpu.PrefetchScalarGridSpec(
            num_scalar_prefetch=1,
            grid=(rows // tile,),
            in_specs=specs,
            out_specs=pl.BlockSpec((tile, wide), lambda i, c: (i, 0)),
        ),
        cost_estimate=pl.CostEstimate(
            flops=6 * rows * depth * wide,
            bytes_accessed=4 * rows * (depth + 2 * wide),
            transcendentals=0,
        ),
        name="apply_chunk",
    )(index, *args)


def update_kernel(order_ref, a_ref, near_ref, far_ref, vr_ref, vc_ref, zc_ref, *rest):
    out_ref, right = rest[-2:]

    @pl.when(pl.program_id(0) == 0)
    def _():
        v_high, v_low = halves(vc_ref[...])
        z_high, z_low = halves(zc_ref[...])
        right[...] = jnp.concatenate([v_high, v_high, v_low, z_high, z_high, z_low], axis=1)

    first = pl.program_id(0) < pl.num_programs(0) // 2
    w_high, w_low = halves(jnp.where(first, near_ref[...], far_ref[...]))
    v_high, v_low = halves(vr_ref[...])
    left = jnp.concatenate([w_high, w_low, w_high, v_high, v_low, v_high], axis=1)
    out_ref[...] = a_ref[...] - lax.dot_general(
        left, right[...], (((1,), (1,)), ((), ())), preferred_element_type=jnp.float32
    )


def update_chunk(matrix, w_near, w_far, v_row, v_chunk, z_chunk, order, out):
    rows, (depth, wide) = matrix.shape[0], v_chunk.shape
    steps = order.shape[0] - 1
    tile, half = rows // steps, steps // 2
    specs = [
        pl.BlockSpec((tile, depth), lambda i, c: (c[i + 1], c[0])),
        pl.BlockSpec((tile, wide), lambda i, c: (jnp.minimum(i, half - 1), 0)),
        pl.BlockSpec((tile, wide), lambda i, c: (jnp.maximum(i - half, 0), 0)),
        pl.BlockSpec((tile, wide), lambda i, c: (c[i + 1], 0)),
        pl.BlockSpec((depth, wide), lambda i, c: (0, 0)),
        pl.BlockSpec((depth, wide), lambda i, c: (0, 0)),
    ]
    args = [matrix, w_near, w_far, v_row, v_chunk, z_chunk]
    alias = {}
    if out is not None:
        specs.append(pl.BlockSpec(memory_space=pl.ANY))
        args.append(out)
        alias = {7: 0}
    return pl.pallas_call(
        update_kernel,
        out_shape=jax.ShapeDtypeStruct(matrix.shape, jnp.float32),
        grid_spec=pltpu.PrefetchScalarGridSpec(
            num_scalar_prefetch=1,
            grid=(steps,),
            in_specs=specs,
            out_specs=pl.BlockSpec((tile, depth), lambda i, c: (c[i + 1], c[0])),
            scratch_shapes=[pltpu.VMEM((depth, 6 * wide), jnp.bfloat16)],
        ),
        input_output_aliases=alias,
        cost_estimate=pl.CostEstimate(
            flops=12 * rows * depth * wide,
            bytes_accessed=8 * rows * (depth + wide),
            transcendentals=0,
        ),
        name="update_chunk",
    )(order, *args)


def dot(a, b):
    return jnp.dot(a, b, precision=lax.Precision.HIGH, preferred_element_type=jnp.float32)


def swap(x, axis, bit):
    count = lax.axis_size(axis)
    return lax.ppermute(x, axis, [(i, i ^ bit) for i in range(count)])


def pick(x, index, axis):
    return lax.dynamic_index_in_dim(x, index, axis, keepdims=False)


def scatter_sum(total):
    if lax.axis_size("col") != 4 or lax.axis_size("grp") != 2:
        return lax.psum_scatter(total, ("col", "grp"), scatter_dimension=0, tiled=True)
    col, y = lax.axis_index("col"), lax.axis_index("grp")
    x, core = col // 2, col % 2
    depth, wide = total.shape[0] // 8, total.shape[1]
    total = total.reshape(2, 2, 2, depth, wide)
    mine = pick(total, core, 1) + swap(pick(total, 1 - core, 1), "col", 1)
    near, far = mine[:, :, : depth // 2], mine[:, :, depth // 2 :]
    near_in = swap(pick(near, 1 - x, 0), "col", 2)
    far_in = swap(pick(far, 1 - y, 1), "grp", 1)
    near = pick(near, x, 0) + near_in
    far = pick(far, y, 1) + far_in
    near_in = swap(pick(near, 1 - y, 0), "grp", 1)
    far_in = swap(pick(far, 1 - x, 0), "col", 2)
    return jnp.concatenate([pick(near, y, 0) + near_in, pick(far, x, 0) + far_in], axis=0)


def gather_rows(own):
    if lax.axis_size("col") != 4 or lax.axis_size("grp") != 2:
        whole = lax.all_gather(own, ("col", "grp"), axis=0, tiled=True)
        half = whole.shape[0] // 2
        tiles = jnp.arange(whole.shape[0] // own.shape[0])
        return whole[:half], whole[half:], tiles
    depth, _ = own.shape
    near, far = own[None, : depth // 2], own[None, depth // 2 :]
    near = jnp.concatenate([near, swap(near, "grp", 1)])
    far = jnp.concatenate([far, swap(far, "col", 2)])
    near_in, far_in = swap(near, "col", 2), swap(far, "grp", 1)
    near = jnp.concatenate([near, near_in])
    tiles = []
    for tile in range(4):
        source, place = (far, far_in)[tile % 2], tile // 2
        tiles += [near[tile], source[place]]
    mine = jnp.concatenate(tiles, axis=0)
    col, y = lax.axis_index("col"), lax.axis_index("grp")
    bits = jnp.arange(8)
    cols = col ^ (2 * (bits // 2 % 2) + bits // 4)
    rest = swap(mine, "col", 1)
    return mine, rest, cols * 2 + (y ^ (bits % 2))


def ring_step(matrix, basis_rows, reflectors, tfactor):
    plane = ("col", "grp")
    member, groups = lax.axis_index(plane), lax.axis_size(plane)
    row, count = lax.axis_index("row"), lax.axis_size("row")
    ring = [(i, (i + 1) % count) for i in range(count)]
    slice_rows = reflectors.shape[0] // groups
    own_v = lax.dynamic_slice_in_dim(reflectors, member * slice_rows, slice_rows, 0)

    v_chunks, owners = [own_v], []
    for step in range(count):
        owners.append(((row - step + count) % count).astype(jnp.int32).reshape(1))
        if step + 1 < count:
            v_chunks.append(lax.ppermute(v_chunks[-1], "row", ring))
    total = apply_chunk(matrix, own_v, None, owners[0])
    total, q_proj = lax.optimization_barrier((total, dot(basis_rows, reflectors)))
    q_proj = lax.psum(q_proj, "row")
    for chunk, owner in zip(v_chunks[1:], owners[1:]):
        total = apply_chunk(matrix, chunk, total, owner)

    cross, total = lax.optimization_barrier((dot(reflectors.T, total), total))
    cross = lax.psum_scatter(cross, plane, scatter_dimension=0, tiled=True)
    applied = scatter_sum(total)
    w_slice = dot(applied, tfactor)
    cross, w_slice = lax.optimization_barrier((cross, w_slice))
    cross = lax.all_gather(lax.psum(cross, "row"), plane, axis=0, tiled=True)
    w_chunks = [w_slice]
    for _ in range(count - 1):
        w_chunks.append(lax.ppermute(w_chunks[-1], "row", ring))
    w_near, w_far, tiles = gather_rows(w_slice)
    inner = dot(tfactor.T, dot(cross, tfactor))

    out = None
    for v_chunk, w_chunk, owner in zip(v_chunks, w_chunks, owners):
        if out is not None:
            out, w_chunk = lax.optimization_barrier((out, w_chunk))
        z_chunk = w_chunk - dot(v_chunk, inner.T)
        order = jnp.concatenate([owner, tiles.astype(jnp.int32)])
        out = update_chunk(matrix, w_near, w_far, reflectors, v_chunk, z_chunk, order, out)

    new_basis = basis_rows - dot(dot(q_proj, tfactor), reflectors.T)
    return (out, new_basis)


def project_kernel(index_ref, a_ref, v_ref, out_ref):
    a_high, a_low = halves(a_ref[...])
    v_high, v_low = halves(v_ref[...])
    product = lax.dot_general(
        jnp.concatenate([a_high, a_low, a_high], axis=0),
        jnp.concatenate([v_high, v_high, v_low], axis=0),
        (((0,), (0,)), ((), ())),
        preferred_element_type=jnp.float32,
    )

    @pl.when(pl.program_id(0) == 0)
    def _():
        out_ref[...] = product

    @pl.when(pl.program_id(0) > 0)
    def _():
        out_ref[...] += product


def project(matrix, reflectors, index, depth):
    rows, wide = reflectors.shape
    tile = min(1024, rows)
    return pl.pallas_call(
        project_kernel,
        out_shape=jax.ShapeDtypeStruct((depth, wide), jnp.float32),
        grid_spec=pltpu.PrefetchScalarGridSpec(
            num_scalar_prefetch=1,
            grid=(rows // tile,),
            in_specs=[
                pl.BlockSpec((tile, depth), lambda i, c: (i, c[0])),
                pl.BlockSpec((tile, wide), lambda i, c: (i, 0)),
            ],
            out_specs=pl.BlockSpec((depth, wide), lambda i, c: (0, 0)),
        ),
        cost_estimate=pl.CostEstimate(
            flops=6 * rows * depth * wide,
            bytes_accessed=4 * rows * (depth + wide),
            transcendentals=0,
        ),
        name="project",
    )(index, matrix, reflectors)


def tdot(a, b):
    return lax.dot_general(
        a, b, (((0,), (0,)), ((), ())), precision=lax.Precision.HIGH, preferred_element_type=jnp.float32
    )


def scalar(x):
    return x.astype(jnp.int32).reshape(1)


def send(x, pairs):
    return lax.ppermute(x, "row", pairs)


OUTER, INNER, FINAL = [(0, 1), (3, 2)], [(1, 2), (2, 1)], [(2, 3), (1, 0)]
UP, DOWN = [(0, 1), (1, 2), (2, 3)], [(3, 2), (2, 1), (1, 0)]
UP2, DOWN2 = [(1, 2), (2, 3)], [(2, 1), (1, 0)]


def total_sum(x):
    bits = (("col", 1), ("col", 2), ("grp", 1))
    here = [(lax.axis_index(axis) // bit) % 2 for axis, bit in bits]
    for (axis, bit), at in zip(bits, here):
        x = x.reshape(2, x.shape[0] // 2, x.shape[1])
        x = pick(x, at, 0) + swap(pick(x, 1 - at, 0), axis, bit)
    for bit in (1, 2):
        x = x + swap(x, "row", bit)
    for (axis, bit), at in reversed(list(zip(bits, here))):
        other = swap(x, axis, bit)
        x = jnp.where(at == 0, jnp.concatenate([x, other]), jnp.concatenate([other, x]))
    return x


def spread(own):
    up, down = send(own, UP), send(own, DOWN)
    two = send(up, UP2) + send(down, DOWN2)
    return up, down, two


def arranged(up, down, two, last, z):
    first = jnp.where(z == 3, up, down)
    third = jnp.where((z == 0) | (z == 3), last, up)
    return first, two, third


def line_step(matrix, basis_rows, reflectors, tfactor):
    z = lax.axis_index("row")
    member, groups = lax.axis_index(("col", "grp")), lax.axis_size(("col", "grp"))
    depth = reflectors.shape[0] // groups
    own_v = lax.dynamic_slice_in_dim(reflectors, member * depth, depth, 0)

    v_up, v_down, v_two = spread(own_v)
    v_last = send(v_two, FINAL)

    low = z < 2
    early, late = jnp.where(low, z + 3, z + 1) % 4, jnp.where(low, z + 1, z + 3) % 4
    first = project(matrix, reflectors, scalar(early), depth)
    outer1 = send(first, OUTER)
    first, at = lax.optimization_barrier((first, scalar((z + 2) % 4)))
    middle = project(matrix, reflectors, at, depth)
    outer2 = send(middle, OUTER)
    middle, at = lax.optimization_barrier((middle, scalar(late)))
    second = project(matrix, reflectors, at, depth)
    outer3 = send(second, OUTER)
    second, at = lax.optimization_barrier((second, scalar(z)))
    same = project(matrix, reflectors, at, depth)
    inner2 = send(middle + outer1, INNER)
    inner3 = send(second + outer2, INNER)
    final3 = send(first + inner2, FINAL)

    same, basis = lax.optimization_barrier((same, basis_rows))
    q_proj = dot(basis, reflectors)

    above = jnp.where(z == 3, v_last, v_down)
    pair = tdot(above, jnp.where(low, second, first))
    cross = tdot(own_v, same) + tdot(v_two, middle) + pair + pair.T
    cross = total_sum(cross)
    inner = dot(tfactor.T, dot(cross, tfactor))

    applied = same + outer3 + inner3 + final3
    w_slice = dot(applied, tfactor)
    w_slice, q_proj = lax.optimization_barrier((w_slice, q_proj))
    w_up, w_down, w_two = spread(w_slice)
    w_last = send(w_two, FINAL)
    w_near, w_far, tiles = gather_rows(w_slice)

    q_pair = q_proj + send(q_proj, OUTER)
    q_full = q_pair + send(q_pair, INNER)
    q_full = jnp.where((z == 1) | (z == 2), q_full, send(q_full, FINAL))

    near = jnp.where(z == 3, 2, z + 1)
    over = (z + 2) % 4
    owners = [z, near, over, 6 - z - near - over]
    v_chunks = [own_v, *arranged(v_up, v_down, v_two, v_last, z)]
    w_chunks = [w_slice, *arranged(w_up, w_down, w_two, w_last, z)]
    out = None
    for v_chunk, w_chunk, owner in zip(v_chunks, w_chunks, owners):
        if out is not None:
            out, w_chunk = lax.optimization_barrier((out, w_chunk))
        z_chunk = w_chunk - dot(v_chunk, inner.T)
        order = jnp.concatenate([scalar(owner), tiles.astype(jnp.int32)])
        out = update_chunk(matrix, w_near, w_far, reflectors, v_chunk, z_chunk, order, out)

    out, q_full = lax.optimization_barrier((out, q_full))
    new_basis = basis_rows - dot(dot(q_full, tfactor), reflectors.T)
    return (out, new_basis)


def on_device(*args):
    sizes = tuple(lax.axis_size(name) for name in ("row", "col", "grp"))
    return (line_step if sizes == (4, 4, 2) else ring_step)(*args)


def solution(mesh):
    placed = (P("row", ("col", "grp")), P(("col", "grp"), "row"), P("row", None), P())
    return jax.shard_map(
        on_device,
        mesh=mesh,
        in_specs=placed,
        out_specs=(P("row", ("col", "grp")), P(("col", "grp"), "row")),
        check_vma=False,
    )
```

```python
import jax
import jax.numpy as jnp
from jax import lax
from jax.experimental import pallas as pl
from jax.experimental.pallas import tpu as pltpu
from jax.sharding import PartitionSpec as P


def halves(x):
    high = x.astype(jnp.bfloat16)
    return high, (x - high.astype(jnp.float32)).astype(jnp.bfloat16)


def apply_kernel(index_ref, a_ref, v_ref, *rest):
    out_ref = rest[-1]
    a_high, a_low = halves(a_ref[...])
    v_high, v_low = halves(v_ref[...])
    product = jnp.dot(
        jnp.concatenate([a_high, a_low, a_high], axis=1),
        jnp.concatenate([v_high, v_high, v_low], axis=0),
        preferred_element_type=jnp.float32,
    )
    out_ref[...] = product if len(rest) == 1 else rest[0][...] + product


def apply_chunk(matrix, chunk, total, index):
    rows, (depth, wide) = matrix.shape[0], chunk.shape
    tile = min(512, rows)
    specs = [
        pl.BlockSpec((tile, depth), lambda i, c: (i, c[0])),
        pl.BlockSpec((depth, wide), lambda i, c: (0, 0)),
    ]
    args = [matrix, chunk]
    if total is not None:
        specs.append(pl.BlockSpec((tile, wide), lambda i, c: (i, 0)))
        args.append(total)
    return pl.pallas_call(
        apply_kernel,
        out_shape=jax.ShapeDtypeStruct((rows, wide), jnp.float32),
        grid_spec=pltpu.PrefetchScalarGridSpec(
            num_scalar_prefetch=1,
            grid=(rows // tile,),
            in_specs=specs,
            out_specs=pl.BlockSpec((tile, wide), lambda i, c: (i, 0)),
        ),
        cost_estimate=pl.CostEstimate(
            flops=6 * rows * depth * wide,
            bytes_accessed=4 * rows * (depth + 2 * wide),
            transcendentals=0,
        ),
        name="apply_chunk",
    )(index, *args)


def update_kernel(order_ref, a_ref, near_ref, far_ref, vr_ref, vc_ref, zc_ref, *rest):
    out_ref, right = rest[-2:]

    @pl.when(pl.program_id(0) == 0)
    def _():
        v_high, v_low = halves(vc_ref[...])
        z_high, z_low = halves(zc_ref[...])
        right[...] = jnp.concatenate([v_high, v_high, v_low, z_high, z_high, z_low], axis=1)

    first = pl.program_id(0) < pl.num_programs(0) // 2
    w_high, w_low = halves(jnp.where(first, near_ref[...], far_ref[...]))
    v_high, v_low = halves(vr_ref[...])
    left = jnp.concatenate([w_high, w_low, w_high, v_high, v_low, v_high], axis=1)
    out_ref[...] = a_ref[...] - lax.dot_general(
        left, right[...], (((1,), (1,)), ((), ())), preferred_element_type=jnp.float32
    )


def update_chunk(matrix, w_near, w_far, v_row, v_chunk, z_chunk, order, out):
    rows, (depth, wide) = matrix.shape[0], v_chunk.shape
    steps = order.shape[0] - 1
    tile, half = rows // steps, steps // 2
    specs = [
        pl.BlockSpec((tile, depth), lambda i, c: (c[i + 1], c[0])),
        pl.BlockSpec((tile, wide), lambda i, c: (jnp.minimum(i, half - 1), 0)),
        pl.BlockSpec((tile, wide), lambda i, c: (jnp.maximum(i - half, 0), 0)),
        pl.BlockSpec((tile, wide), lambda i, c: (c[i + 1], 0)),
        pl.BlockSpec((depth, wide), lambda i, c: (0, 0)),
        pl.BlockSpec((depth, wide), lambda i, c: (0, 0)),
    ]
    args = [matrix, w_near, w_far, v_row, v_chunk, z_chunk]
    alias = {}
    if out is not None:
        specs.append(pl.BlockSpec(memory_space=pl.ANY))
        args.append(out)
        alias = {7: 0}
    return pl.pallas_call(
        update_kernel,
        out_shape=jax.ShapeDtypeStruct(matrix.shape, jnp.float32),
        grid_spec=pltpu.PrefetchScalarGridSpec(
            num_scalar_prefetch=1,
            grid=(steps,),
            in_specs=specs,
            out_specs=pl.BlockSpec((tile, depth), lambda i, c: (c[i + 1], c[0])),
            scratch_shapes=[pltpu.VMEM((depth, 6 * wide), jnp.bfloat16)],
        ),
        input_output_aliases=alias,
        cost_estimate=pl.CostEstimate(
            flops=12 * rows * depth * wide,
            bytes_accessed=8 * rows * (depth + wide),
            transcendentals=0,
        ),
        name="update_chunk",
    )(order, *args)


def dot(a, b):
    return jnp.dot(a, b, precision=lax.Precision.HIGH, preferred_element_type=jnp.float32)


def swap(x, axis, bit):
    count = lax.axis_size(axis)
    return lax.ppermute(x, axis, [(i, i ^ bit) for i in range(count)])


def pick(x, index, axis):
    return lax.dynamic_index_in_dim(x, index, axis, keepdims=False)


def scatter_sum(total):
    if lax.axis_size("col") != 4 or lax.axis_size("grp") != 2:
        return lax.psum_scatter(total, ("col", "grp"), scatter_dimension=0, tiled=True)
    col, y = lax.axis_index("col"), lax.axis_index("grp")
    x, core = col // 2, col % 2
    depth, wide = total.shape[0] // 8, total.shape[1]
    total = total.reshape(2, 2, 2, depth, wide)
    mine = pick(total, core, 1) + swap(pick(total, 1 - core, 1), "col", 1)
    near, far = mine[:, :, : depth // 2], mine[:, :, depth // 2 :]
    near_in = swap(pick(near, 1 - x, 0), "col", 2)
    far_in = swap(pick(far, 1 - y, 1), "grp", 1)
    near = pick(near, x, 0) + near_in
    far = pick(far, y, 1) + far_in
    near_in = swap(pick(near, 1 - y, 0), "grp", 1)
    far_in = swap(pick(far, 1 - x, 0), "col", 2)
    return jnp.concatenate([pick(near, y, 0) + near_in, pick(far, x, 0) + far_in], axis=0)


def gather_rows(own):
    if lax.axis_size("col") != 4 or lax.axis_size("grp") != 2:
        whole = lax.all_gather(own, ("col", "grp"), axis=0, tiled=True)
        half = whole.shape[0] // 2
        tiles = jnp.arange(whole.shape[0] // own.shape[0])
        return whole[:half], whole[half:], tiles
    depth, _ = own.shape
    near, far = own[None, : depth // 2], own[None, depth // 2 :]
    near = jnp.concatenate([near, swap(near, "grp", 1)])
    far = jnp.concatenate([far, swap(far, "col", 2)])
    near_in, far_in = swap(near, "col", 2), swap(far, "grp", 1)
    near = jnp.concatenate([near, near_in])
    tiles = []
    for tile in range(4):
        source, place = (far, far_in)[tile % 2], tile // 2
        tiles += [near[tile], source[place]]
    mine = jnp.concatenate(tiles, axis=0)
    col, y = lax.axis_index("col"), lax.axis_index("grp")
    bits = jnp.arange(8)
    cols = col ^ (2 * (bits // 2 % 2) + bits // 4)
    rest = swap(mine, "col", 1)
    return mine, rest, cols * 2 + (y ^ (bits % 2))


def ring_step(matrix, basis_rows, reflectors, tfactor):
    plane = ("col", "grp")
    member, groups = lax.axis_index(plane), lax.axis_size(plane)
    row, count = lax.axis_index("row"), lax.axis_size("row")
    ring = [(i, (i + 1) % count) for i in range(count)]
    slice_rows = reflectors.shape[0] // groups
    own_v = lax.dynamic_slice_in_dim(reflectors, member * slice_rows, slice_rows, 0)

    v_chunks, owners = [own_v], []
    for step in range(count):
        owners.append(((row - step + count) % count).astype(jnp.int32).reshape(1))
        if step + 1 < count:
            v_chunks.append(lax.ppermute(v_chunks[-1], "row", ring))
    total = apply_chunk(matrix, own_v, None, owners[0])
    total, q_proj = lax.optimization_barrier((total, dot(basis_rows, reflectors)))
    q_proj = lax.psum(q_proj, "row")
    for chunk, owner in zip(v_chunks[1:], owners[1:]):
        total = apply_chunk(matrix, chunk, total, owner)

    cross, total = lax.optimization_barrier((dot(reflectors.T, total), total))
    cross = lax.psum_scatter(cross, plane, scatter_dimension=0, tiled=True)
    applied = scatter_sum(total)
    w_slice = dot(applied, tfactor)
    cross, w_slice = lax.optimization_barrier((cross, w_slice))
    cross = lax.all_gather(lax.psum(cross, "row"), plane, axis=0, tiled=True)
    w_chunks = [w_slice]
    for _ in range(count - 1):
        w_chunks.append(lax.ppermute(w_chunks[-1], "row", ring))
    w_near, w_far, tiles = gather_rows(w_slice)
    inner = dot(tfactor.T, dot(cross, tfactor))

    out = None
    for v_chunk, w_chunk, owner in zip(v_chunks, w_chunks, owners):
        if out is not None:
            out, w_chunk = lax.optimization_barrier((out, w_chunk))
        z_chunk = w_chunk - dot(v_chunk, inner.T)
        order = jnp.concatenate([owner, tiles.astype(jnp.int32)])
        out = update_chunk(matrix, w_near, w_far, reflectors, v_chunk, z_chunk, order, out)

    new_basis = basis_rows - dot(dot(q_proj, tfactor), reflectors.T)
    return (out, new_basis)


MESH = pl.DeviceIdType.MESH
INNER, FINAL, OUTER = [(1, 2), (2, 1)], [(2, 3), (1, 0)], [(0, 1), (3, 2)]


def triple(a, b, dims):
    a_high, a_low = halves(a)
    b_high, b_low = halves(b)
    (left,), (right,) = dims
    return lax.dot_general(
        jnp.concatenate([a_high, a_low, a_high], axis=left),
        jnp.concatenate([b_high, b_high, b_low], axis=right),
        (dims, ((), ())),
        preferred_element_type=jnp.float32,
    )


def front_kernel(
    a_hbm, v_hbm, own_hbm, b_hbm, t_ref,
    v_all, w_all, w_rows, q_out, cross_out,
    a_buf, b_buf, v_buf, own, part, outer_in, inner_in, final_in, w_own, q_acc, total,
    half_in, quarter_in, eighth_in, line_in, far_in,
    a_sem, b_sem, v_sem, local_sem, send_sem, recv_sem,
):
    z, col, y = (lax.axis_index(name) for name in ("row", "col", "grp"))
    core, x = lax.rem(col, 2), lax.div(col, 2)
    depth = own.shape[0]
    tile = a_buf.shape[1]
    steps = v_buf.shape[0] // tile
    low = z < 2
    edge = (z == 0) | (z == 3)
    near = jnp.where(low, 1, 2)
    outward = jnp.where(low, 0, 3)
    across = jnp.where(low, 2, 1)
    beside = z + 1 - 2 * lax.rem(z, 2)
    dests = [jnp.where(low, 3, 0), jnp.where(low, 2, 1), beside, z]
    partner = {"row": z, "col": col, "grp": y}
    by_core = partner | {"col": col + 1 - 2 * core}
    by_x = partner | {"col": core + 2 * (1 - x)}
    by_y = partner | {"grp": 1 - y}

    def along(where):
        return partner | {"row": where}

    barrier = pltpu.get_barrier_semaphore()
    for target in (by_core, by_x, by_y, along(lax.rem(z + 1, 4)), along(lax.rem(z + 2, 4)), along(lax.rem(z + 3, 4))):
        pl.semaphore_signal(barrier, inc=1, device_id=target, device_id_type=MESH)
    pl.semaphore_wait(barrier, 6)

    def remote(slot, source, target_ref, target):
        return pltpu.make_async_remote_copy(
            src_ref=source, dst_ref=target_ref, send_sem=send_sem.at[slot], recv_sem=recv_sem.at[slot],
            device_id=target, device_id_type=MESH,
        )

    def spread(base, source, slots):
        return {
            "in": remote(base, source, slots.at[1], along(near)),
            "out": remote(base + 1, source, slots.at[0], along(outward)),
            "over": remote(base + 2, source, slots.at[0], along(across)),
            "out2": remote(base + 3, slots.at[0], slots.at[1], along(outward)),
            "over2": remote(base + 4, slots.at[1], slots.at[2], along(across)),
            "out3": remote(base + 5, slots.at[2], slots.at[2], along(outward)),
        }

    def fetch_a(index, step, slot):
        columns = pl.ds(pl.multiple_of(index * depth, depth), depth)
        rows = pl.ds(pl.multiple_of(step * tile, tile), tile)
        return pltpu.make_async_copy(a_hbm.at[rows, columns], a_buf.at[slot], a_sem.at[slot])

    def fetch_b(step, slot):
        columns = pl.ds(pl.multiple_of(step * tile, tile), tile)
        return pltpu.make_async_copy(b_hbm.at[:, columns], b_buf.at[slot], b_sem.at[slot])

    def fetch_v(step):
        rows = pl.ds(pl.multiple_of(step * tile, tile), tile)
        return pltpu.make_async_copy(v_hbm.at[rows, :], v_buf.at[rows, :], v_sem.at[step])

    gather_v = spread(0, own_hbm, v_all)
    gather_w = spread(6, w_own, w_all)

    @pl.when(edge)
    def _():
        gather_v["in"].start()

    @pl.when(jnp.logical_not(edge))
    def _():
        gather_v["over"].start()
        gather_v["out"].start()

    fetch_a(dests[0], 0, 0).start()
    fetch_v(0).start()
    for step in range(1, steps):
        fetch_v(step).start()
    fetch_own = pltpu.make_async_copy(own_hbm, own, local_sem.at[0])
    fetch_own.start()

    outer = [remote(12 + i, part.at[i], outer_in.at[i], along(near)) for i in range(3)]
    inner = [remote(15 + i, outer_in.at[i], inner_in.at[i], along(across)) for i in range(2)]
    final = remote(17, inner_in.at[0], final_in, along(outward))

    def product(i):
        def body(step, carry):
            slot = lax.rem(step, 2)
            if i == 0:
                fetch_v(step).wait()
            following = dests[i + 1] if i < 3 else dests[i]
            index = jnp.where(step < steps - 1, dests[i], following)
            ahead = lax.rem(step + 1, steps)
            if i < 3:
                fetch_a(index, ahead, 1 - slot).start()
            else:
                @pl.when(step < steps - 1)
                def _():
                    fetch_a(index, ahead, 1 - slot).start()
            fetch_a(dests[i], step, slot).wait()
            rows = pl.ds(pl.multiple_of(step * tile, tile), tile)
            value = triple(a_buf[slot], v_buf[rows, :], ((0,), (0,)))

            @pl.when(step == 0)
            def _():
                part[i] = value

            @pl.when(step > 0)
            def _():
                part[i] += value

            return carry

        lax.fori_loop(0, steps, body, 0)

    for i in range(3):
        product(i)

        @pl.when(edge)
        def _():
            outer[i].start()

        if i == 1:
            @pl.when(jnp.logical_not(edge))
            def _():
                gather_v["over"].wait_recv()
                gather_v["out2"].start()
                gather_v["in"].wait_recv()
                gather_v["over2"].start()

    @pl.when(jnp.logical_not(edge))
    def _():
        outer[0].wait_recv()
        outer_in[0] += part[0]
        inner[0].start()

    fetch_b(0, 0).start()
    product(3)

    @pl.when(jnp.logical_not(edge))
    def _():
        gather_v["over2"].wait_recv()
        gather_v["out3"].start()
        outer[1].wait_recv()
        outer_in[1] += part[1]
        inner[1].start()

    def project_b(step, carry):
        slot = lax.rem(step, 2)

        @pl.when(step < steps - 1)
        def _():
            fetch_b(step + 1, 1 - slot).start()

        fetch_b(step, slot).wait()
        rows = pl.ds(pl.multiple_of(step * tile, tile), tile)
        value = triple(b_buf[slot], v_buf[rows, :], ((1,), (0,)))

        @pl.when(step == 0)
        def _():
            q_acc[...] = value

        @pl.when(step > 0)
        def _():
            q_acc[...] += value

        return carry

    @pl.when(jnp.logical_not(edge))
    def _():
        inner[0].wait_recv()
        inner_in[0] += part[2]
        final.start()

    lax.fori_loop(0, steps, project_b, 0)
    put_q = pltpu.make_async_copy(q_acc, q_out, local_sem.at[1])
    put_q.start()

    @pl.when(jnp.logical_not(edge))
    def _():
        inner[1].wait_recv()
        part[3] += inner_in[1]
        outer[2].wait_recv()
        part[3] += outer_in[2]

    @pl.when(edge)
    def _():
        final.wait_recv()
        part[3] += final_in[...]

    w_own[...] = triple(part[3], t_ref[...], ((1,), (0,)))

    half = depth // 2
    places = [pl.ds(i * depth, half) for i in range(8)], [pl.ds(i * depth + half, half) for i in range(8)]
    top, bottom = pl.ds(0, half), pl.ds(half, half)
    hops = [
        remote(18, w_own.at[top], w_rows.at[places[0][1]], by_y),
        remote(19, w_own.at[bottom], w_rows.at[places[1][2]], by_x),
        remote(20, w_own.at[top], w_rows.at[places[0][2]], by_x),
        remote(21, w_own.at[bottom], w_rows.at[places[1][1]], by_y),
        remote(22, w_rows.at[places[0][1]], w_rows.at[places[0][3]], by_x),
        remote(23, w_rows.at[places[1][2]], w_rows.at[places[1][3]], by_y),
    ]
    shares = [remote(24, w_own, w_rows.at[pl.ds(4 * depth, depth)], by_core)]
    for slot, (side, i) in enumerate([(0, 1), (1, 2), (0, 2), (1, 1), (0, 3), (1, 3)]):
        shares.append(remote(25 + slot, w_rows.at[places[side][i]], w_rows.at[places[side][4 + i]], by_core))

    for hop in hops[:2]:
        hop.start()

    total[...] = triple(own_value(fetch_own, own), part[3], ((0,), (0,)))

    def piece(start, size):
        return pl.ds(pl.multiple_of(start, size), size)

    sizes = [depth // 2, depth // 4, depth // 8]
    bits, targets, landings = [core, x, y], [by_core, by_x, by_y], [half_in, quarter_in, eighth_in]
    base = 0
    reduces = []
    for i in range(3):
        other = base + (1 - bits[i]) * sizes[i]
        base = base + bits[i] * sizes[i]
        copy = remote(31 + i, total.at[piece(other, sizes[i])], landings[i], targets[i])
        copy.start()
        copy.wait_recv()
        here = piece(base, sizes[i])
        total[here, :] += landings[i][...]
        reduces.append(copy)
    mine = piece(base, sizes[2])
    line = [
        remote(34, total.at[mine], line_in, along(beside)),
        remote(35, eighth_in, far_in, along(lax.rem(z + 2, 4))),
    ]
    line[0].start()

    @pl.when(edge)
    def _():
        gather_w["in"].start()

    @pl.when(jnp.logical_not(edge))
    def _():
        gather_w["over"].start()
        gather_w["out"].start()

    shares[0].start()
    hops[2].start()
    hops[3].start()
    put_w = pltpu.make_async_copy(w_own, w_rows.at[pl.ds(0, depth)], local_sem.at[2])
    put_w.start()

    line[0].wait()
    eighth_in[...] = total[mine, :] + line_in[...]
    line[1].start()

    for i in range(2):
        hops[i].wait_recv()
        hops[4 + i].start()
        shares[1 + i].start()

    line[1].wait()
    eighth_in[...] += far_in[...]
    put_c = pltpu.make_async_copy(eighth_in, cross_out.at[mine], local_sem.at[3])
    put_c.start()
    put_c.wait()
    returns = []
    for i in (2, 1, 0):
        here = piece(base - lax.rem(base, sizes[i]), sizes[i])
        copy = remote(36 + i, cross_out.at[here], cross_out.at[here], targets[i])
        copy.start()
        copy.wait_recv()
        returns.append(copy)

    @pl.when(jnp.logical_not(edge))
    def _():
        gather_w["over"].wait_recv()
        gather_w["out2"].start()
        gather_w["in"].wait_recv()
        gather_w["over2"].start()

    for i in range(2, 6):
        hops[i].wait_recv()
        shares[1 + i].start()
    for copy in hops + shares + reduces + returns:
        copy.wait_send()
    for copy in shares:
        copy.wait_recv()
    put_w.wait()
    put_q.wait()

    @pl.when(edge)
    def _():
        gather_v["in"].wait_send()
        gather_w["in"].wait_send()
        for copy in outer:
            copy.wait_send()
        for name in ("out", "out2", "out3"):
            gather_v[name].wait_recv()
        for name in ("out", "out2"):
            gather_w[name].wait_recv()

    @pl.when(jnp.logical_not(edge))
    def _():
        for name in ("over", "out", "out2", "over2", "out3"):
            gather_v[name].wait_send()
        for name in ("over", "out", "out2", "over2"):
            gather_w[name].wait_send()
        for copy in inner + [final]:
            copy.wait_send()
        gather_w["over2"].wait_recv()


def own_value(fetch, own):
    fetch.wait()
    return own[...]


def front(matrix, reflectors, own_v, basis_rows, tfactor):
    depth, wide = own_v.shape
    rows = reflectors.shape[0]
    tile = rows // 4
    hbm = pl.BlockSpec(memory_space=pltpu.HBM)
    chunk = (depth, wide)

    def shape(*dims):
        return jax.ShapeDtypeStruct(dims, jnp.float32)

    def vmem(*dims):
        return pltpu.VMEM(dims, jnp.float32)

    return pl.pallas_call(
        front_kernel,
        out_shape=[shape(3, *chunk), shape(3, *chunk), shape(8 * depth, wide), shape(*chunk), shape(*chunk)],
        in_specs=[hbm] * 4 + [pl.BlockSpec(memory_space=pltpu.VMEM)],
        out_specs=[hbm] * 5,
        scratch_shapes=[
            vmem(2, tile, depth), vmem(2, depth, tile), vmem(rows, wide), vmem(*chunk), vmem(4, *chunk),
            vmem(3, *chunk), vmem(2, *chunk), vmem(*chunk), vmem(*chunk), vmem(*chunk), vmem(*chunk),
            vmem(depth // 2, wide), vmem(depth // 4, wide), vmem(depth // 8, wide), vmem(depth // 8, wide),
            vmem(depth // 8, wide),
            pltpu.SemaphoreType.DMA((2,)), pltpu.SemaphoreType.DMA((2,)), pltpu.SemaphoreType.DMA((4,)),
            pltpu.SemaphoreType.DMA((4,)), pltpu.SemaphoreType.DMA((39,)), pltpu.SemaphoreType.DMA((39,)),
        ],
        compiler_params=pltpu.CompilerParams(
            collective_id=0, has_side_effects=True, vmem_limit_bytes=60 * 1024 * 1024
        ),
        cost_estimate=pl.CostEstimate(
            flops=30 * rows * depth * wide, bytes_accessed=20 * rows * depth, transcendentals=0
        ),
        name="front",
    )(matrix, reflectors, own_v, basis_rows, tfactor)


def finish_kernel(order_ref, a_ref, w_ref, v_ref, vc_ref, wc_ref, y_ref, *rest):
    out_ref, right = rest[-2:]

    @pl.when(pl.program_id(0) == 0)
    def _():
        chunk = vc_ref[...]
        z_high, z_low = halves(wc_ref[...] - triple(chunk, y_ref[...], ((1,), (1,))))
        v_high, v_low = halves(chunk)
        right[...] = jnp.concatenate([v_high, v_high, v_low, z_high, z_high, z_low], axis=1)

    w_high, w_low = halves(w_ref[...])
    v_high, v_low = halves(v_ref[...])
    left = jnp.concatenate([w_high, w_low, w_high, v_high, v_low, v_high], axis=1)
    out_ref[...] = a_ref[...] - lax.dot_general(
        left, right[...], (((1,), (1,)), ((), ())), preferred_element_type=jnp.float32
    )


def finish_chunk(matrix, w_rows, v_row, v_chunks, w_chunks, slots, inner, order, out):
    rows, (depth, wide) = matrix.shape[0], v_chunks.shape[1:]
    tile, steps = depth, rows // depth
    specs = [
        pl.BlockSpec((tile, depth), lambda i, c: (c[i + 1], c[0])),
        pl.BlockSpec((tile, wide), lambda i, c: (i, 0)),
        pl.BlockSpec((tile, wide), lambda i, c: (c[i + 1], 0)),
        pl.BlockSpec((None, depth, wide), lambda i, c: (slots[0], 0, 0)),
        pl.BlockSpec((None, depth, wide), lambda i, c: (slots[1], 0, 0)),
        pl.BlockSpec(inner.shape, lambda i, c: (0, 0)),
    ]
    args = [matrix, w_rows, v_row, v_chunks, w_chunks, inner]
    alias = {}
    if out is not None:
        specs.append(pl.BlockSpec(memory_space=pl.ANY))
        args.append(out)
        alias = {7: 0}
    return pl.pallas_call(
        finish_kernel,
        out_shape=jax.ShapeDtypeStruct(matrix.shape, jnp.float32),
        grid_spec=pltpu.PrefetchScalarGridSpec(
            num_scalar_prefetch=1,
            grid=(steps,),
            in_specs=specs,
            out_specs=pl.BlockSpec((tile, depth), lambda i, c: (c[i + 1], c[0])),
            scratch_shapes=[pltpu.VMEM((depth, 6 * wide), jnp.bfloat16)],
        ),
        input_output_aliases=alias,
        cost_estimate=pl.CostEstimate(
            flops=12 * rows * depth * wide,
            bytes_accessed=8 * rows * (depth + wide),
            transcendentals=0,
        ),
        name="finish_chunk",
    )(order, *args)


def scalar(x):
    return x.astype(jnp.int32).reshape(1)


def send(x, pairs):
    return lax.ppermute(x, "row", pairs)


def line_step(matrix, basis_rows, reflectors, tfactor):
    z, col, y = (lax.axis_index(name) for name in ("row", "col", "grp"))
    member, groups = lax.axis_index(("col", "grp")), lax.axis_size(("col", "grp"))
    depth = reflectors.shape[0] // groups
    own_v = lax.dynamic_slice_in_dim(reflectors, member * depth, depth, 0)
    v_all, w_all, w_rows, q_proj, cross = front(matrix, reflectors, own_v, basis_rows, tfactor)
    inner = dot(tfactor.T, dot(cross, tfactor))

    bits = jnp.arange(8)
    tiles = (col ^ (2 * (bits // 2 % 2) + bits // 4)) * 2 + (y ^ (bits % 2))
    edge, low = (z == 0) | (z == 3), z < 2
    owners = [
        z,
        jnp.where(edge, jnp.where(low, 1, 2), jnp.where(low, 2, 1)),
        jnp.where(edge, jnp.where(low, 2, 1), jnp.where(low, 0, 3)),
        jnp.where(low, 3, 0),
    ]
    w_third = w_all[2]
    w_last = jnp.where(edge, send(w_third, FINAL), w_third)
    q_pair = q_proj + send(q_proj, OUTER)

    out = None
    for i, owner in enumerate(owners):
        order = jnp.concatenate([scalar(owner), tiles.astype(jnp.int32)])
        if i == 2:
            out, q_pair = lax.optimization_barrier((out, q_pair))
            q_full = q_pair + send(q_pair, INNER)
        if i == 3:
            out, q_full, w_last = lax.optimization_barrier((out, q_full, w_last))
            q_full = jnp.where(edge, send(q_full, FINAL), q_full)
        v_from, w_from, slots = v_all, w_all, (i - 1, i - 1)
        if i == 0:
            v_from, w_from, slots = own_v[None], w_rows.reshape(groups, depth, -1), (0, 0)
        if i == 3:
            w_from, slots = w_last[None], (2, 0)
        out = finish_chunk(matrix, w_rows, reflectors, v_from, w_from, slots, inner, order, out)

    out, q_full = lax.optimization_barrier((out, q_full))
    new_basis = basis_rows - dot(dot(q_full, tfactor), reflectors.T)
    return (out, new_basis)


def on_device(*args):
    sizes = tuple(lax.axis_size(name) for name in ("row", "col", "grp"))
    return (line_step if sizes == (4, 4, 2) else ring_step)(*args)


def solution(mesh):
    placed = (P("row", ("col", "grp")), P(("col", "grp"), "row"), P("row", None), P())
    return jax.shard_map(
        on_device,
        mesh=mesh,
        in_specs=placed,
        out_specs=(P("row", ("col", "grp")), P(("col", "grp"), "row")),
        check_vma=False,
    )
```

```python
import functools

import jax
import jax.numpy as jnp
from jax import lax
from jax.experimental import pallas as pl
from jax.experimental.pallas import tpu as pltpu
from jax.sharding import PartitionSpec as P


def halves(x):
    high = x.astype(jnp.bfloat16)
    return high, (x - high.astype(jnp.float32)).astype(jnp.bfloat16)


def apply_kernel(index_ref, a_ref, v_ref, *rest):
    out_ref = rest[-1]
    a_high, a_low = halves(a_ref[...])
    v_high, v_low = halves(v_ref[...])
    product = jnp.dot(
        jnp.concatenate([a_high, a_low, a_high], axis=1),
        jnp.concatenate([v_high, v_high, v_low], axis=0),
        preferred_element_type=jnp.float32,
    )
    out_ref[...] = product if len(rest) == 1 else rest[0][...] + product


def apply_chunk(matrix, chunk, total, index):
    rows, (depth, wide) = matrix.shape[0], chunk.shape
    tile = min(512, rows)
    specs = [
        pl.BlockSpec((tile, depth), lambda i, c: (i, c[0])),
        pl.BlockSpec((depth, wide), lambda i, c: (0, 0)),
    ]
    args = [matrix, chunk]
    if total is not None:
        specs.append(pl.BlockSpec((tile, wide), lambda i, c: (i, 0)))
        args.append(total)
    return pl.pallas_call(
        apply_kernel,
        out_shape=jax.ShapeDtypeStruct((rows, wide), jnp.float32),
        grid_spec=pltpu.PrefetchScalarGridSpec(
            num_scalar_prefetch=1,
            grid=(rows // tile,),
            in_specs=specs,
            out_specs=pl.BlockSpec((tile, wide), lambda i, c: (i, 0)),
        ),
        cost_estimate=pl.CostEstimate(
            flops=6 * rows * depth * wide,
            bytes_accessed=4 * rows * (depth + 2 * wide),
            transcendentals=0,
        ),
        name="apply_chunk",
    )(index, *args)


def update_kernel(order_ref, a_ref, near_ref, far_ref, vr_ref, vc_ref, zc_ref, *rest):
    out_ref, right = rest[-2:]

    @pl.when(pl.program_id(0) == 0)
    def _():
        v_high, v_low = halves(vc_ref[...])
        z_high, z_low = halves(zc_ref[...])
        right[...] = jnp.concatenate([v_high, v_high, v_low, z_high, z_high, z_low], axis=1)

    first = pl.program_id(0) < pl.num_programs(0) // 2
    w_high, w_low = halves(jnp.where(first, near_ref[...], far_ref[...]))
    v_high, v_low = halves(vr_ref[...])
    left = jnp.concatenate([w_high, w_low, w_high, v_high, v_low, v_high], axis=1)
    out_ref[...] = a_ref[...] - lax.dot_general(
        left, right[...], (((1,), (1,)), ((), ())), preferred_element_type=jnp.float32
    )


def update_chunk(matrix, w_near, w_far, v_row, v_chunk, z_chunk, order, out):
    rows, (depth, wide) = matrix.shape[0], v_chunk.shape
    steps = order.shape[0] - 1
    tile, half = rows // steps, steps // 2
    specs = [
        pl.BlockSpec((tile, depth), lambda i, c: (c[i + 1], c[0])),
        pl.BlockSpec((tile, wide), lambda i, c: (jnp.minimum(i, half - 1), 0)),
        pl.BlockSpec((tile, wide), lambda i, c: (jnp.maximum(i - half, 0), 0)),
        pl.BlockSpec((tile, wide), lambda i, c: (c[i + 1], 0)),
        pl.BlockSpec((depth, wide), lambda i, c: (0, 0)),
        pl.BlockSpec((depth, wide), lambda i, c: (0, 0)),
    ]
    args = [matrix, w_near, w_far, v_row, v_chunk, z_chunk]
    alias = {}
    if out is not None:
        specs.append(pl.BlockSpec(memory_space=pl.ANY))
        args.append(out)
        alias = {7: 0}
    return pl.pallas_call(
        update_kernel,
        out_shape=jax.ShapeDtypeStruct(matrix.shape, jnp.float32),
        grid_spec=pltpu.PrefetchScalarGridSpec(
            num_scalar_prefetch=1,
            grid=(steps,),
            in_specs=specs,
            out_specs=pl.BlockSpec((tile, depth), lambda i, c: (c[i + 1], c[0])),
            scratch_shapes=[pltpu.VMEM((depth, 6 * wide), jnp.bfloat16)],
        ),
        input_output_aliases=alias,
        cost_estimate=pl.CostEstimate(
            flops=12 * rows * depth * wide,
            bytes_accessed=8 * rows * (depth + wide),
            transcendentals=0,
        ),
        name="update_chunk",
    )(order, *args)


def dot(a, b):
    return jnp.dot(a, b, precision=lax.Precision.HIGH, preferred_element_type=jnp.float32)


def swap(x, axis, bit):
    count = lax.axis_size(axis)
    return lax.ppermute(x, axis, [(i, i ^ bit) for i in range(count)])


def pick(x, index, axis):
    return lax.dynamic_index_in_dim(x, index, axis, keepdims=False)


def scatter_sum(total):
    if lax.axis_size("col") != 4 or lax.axis_size("grp") != 2:
        return lax.psum_scatter(total, ("col", "grp"), scatter_dimension=0, tiled=True)
    col, y = lax.axis_index("col"), lax.axis_index("grp")
    x, core = col // 2, col % 2
    depth, wide = total.shape[0] // 8, total.shape[1]
    total = total.reshape(2, 2, 2, depth, wide)
    mine = pick(total, core, 1) + swap(pick(total, 1 - core, 1), "col", 1)
    near, far = mine[:, :, : depth // 2], mine[:, :, depth // 2 :]
    near_in = swap(pick(near, 1 - x, 0), "col", 2)
    far_in = swap(pick(far, 1 - y, 1), "grp", 1)
    near = pick(near, x, 0) + near_in
    far = pick(far, y, 1) + far_in
    near_in = swap(pick(near, 1 - y, 0), "grp", 1)
    far_in = swap(pick(far, 1 - x, 0), "col", 2)
    return jnp.concatenate([pick(near, y, 0) + near_in, pick(far, x, 0) + far_in], axis=0)


def gather_rows(own):
    if lax.axis_size("col") != 4 or lax.axis_size("grp") != 2:
        whole = lax.all_gather(own, ("col", "grp"), axis=0, tiled=True)
        half = whole.shape[0] // 2
        tiles = jnp.arange(whole.shape[0] // own.shape[0])
        return whole[:half], whole[half:], tiles
    depth, _ = own.shape
    near, far = own[None, : depth // 2], own[None, depth // 2 :]
    near = jnp.concatenate([near, swap(near, "grp", 1)])
    far = jnp.concatenate([far, swap(far, "col", 2)])
    near_in, far_in = swap(near, "col", 2), swap(far, "grp", 1)
    near = jnp.concatenate([near, near_in])
    tiles = []
    for tile in range(4):
        source, place = (far, far_in)[tile % 2], tile // 2
        tiles += [near[tile], source[place]]
    mine = jnp.concatenate(tiles, axis=0)
    col, y = lax.axis_index("col"), lax.axis_index("grp")
    bits = jnp.arange(8)
    cols = col ^ (2 * (bits // 2 % 2) + bits // 4)
    rest = swap(mine, "col", 1)
    return mine, rest, cols * 2 + (y ^ (bits % 2))


def ring_step(matrix, basis_rows, reflectors, tfactor):
    plane = ("col", "grp")
    member, groups = lax.axis_index(plane), lax.axis_size(plane)
    row, count = lax.axis_index("row"), lax.axis_size("row")
    ring = [(i, (i + 1) % count) for i in range(count)]
    slice_rows = reflectors.shape[0] // groups
    own_v = lax.dynamic_slice_in_dim(reflectors, member * slice_rows, slice_rows, 0)

    v_chunks, owners = [own_v], []
    for step in range(count):
        owners.append(((row - step + count) % count).astype(jnp.int32).reshape(1))
        if step + 1 < count:
            v_chunks.append(lax.ppermute(v_chunks[-1], "row", ring))
    total = apply_chunk(matrix, own_v, None, owners[0])
    total, q_proj = lax.optimization_barrier((total, dot(basis_rows, reflectors)))
    q_proj = lax.psum(q_proj, "row")
    for chunk, owner in zip(v_chunks[1:], owners[1:]):
        total = apply_chunk(matrix, chunk, total, owner)

    cross, total = lax.optimization_barrier((dot(reflectors.T, total), total))
    cross = lax.psum_scatter(cross, plane, scatter_dimension=0, tiled=True)
    applied = scatter_sum(total)
    w_slice = dot(applied, tfactor)
    cross, w_slice = lax.optimization_barrier((cross, w_slice))
    cross = lax.all_gather(lax.psum(cross, "row"), plane, axis=0, tiled=True)
    w_chunks = [w_slice]
    for _ in range(count - 1):
        w_chunks.append(lax.ppermute(w_chunks[-1], "row", ring))
    w_near, w_far, tiles = gather_rows(w_slice)
    inner = dot(tfactor.T, dot(cross, tfactor))

    out = None
    for v_chunk, w_chunk, owner in zip(v_chunks, w_chunks, owners):
        if out is not None:
            out, w_chunk = lax.optimization_barrier((out, w_chunk))
        z_chunk = w_chunk - dot(v_chunk, inner.T)
        order = jnp.concatenate([owner, tiles.astype(jnp.int32)])
        out = update_chunk(matrix, w_near, w_far, reflectors, v_chunk, z_chunk, order, out)

    new_basis = basis_rows - dot(dot(q_proj, tfactor), reflectors.T)
    return (out, new_basis)


MESH = pl.DeviceIdType.MESH
INNER, FINAL = [(1, 2), (2, 1)], [(2, 3), (1, 0)]


def triple(a, b, dims):
    a_high, a_low = halves(a)
    b_high, b_low = halves(b)
    (left,), (right,) = dims
    return lax.dot_general(
        jnp.concatenate([a_high, a_low, a_high], axis=left),
        jnp.concatenate([b_high, b_high, b_low], axis=right),
        (dims, ((), ())),
        preferred_element_type=jnp.float32,
    )


def front_kernel(
    a_hbm, v_hbm, own_hbm, b_hbm, t_ref,
    v_all, w_all, w_rows, q_out, y_out,
    a_buf, b_buf, v_buf, own, part, outer_in, inner_in, final_in, w_own, q_acc, q_in, total, cross, slots,
    half_in, quarter_in, eighth_in, line_in, far_in,
    a_sem, b_sem, v_sem, slot_sem, local_sem, send_sem, recv_sem,
):
    z, col, y = (lax.axis_index(name) for name in ("row", "col", "grp"))
    core, x = lax.rem(col, 2), lax.div(col, 2)
    depth = own.shape[0]
    tile = a_buf.shape[1]
    steps = v_buf.shape[0] // tile
    low = z < 2
    edge = (z == 0) | (z == 3)
    inside = jnp.logical_not(edge)
    near = jnp.where(low, 1, 2)
    outward = jnp.where(low, 0, 3)
    across = jnp.where(low, 2, 1)
    beside = z + 1 - 2 * lax.rem(z, 2)
    dests = [jnp.where(low, 3, 0), jnp.where(low, 2, 1), beside, z]
    partner = {"row": z, "col": col, "grp": y}
    by_core = partner | {"col": col + 1 - 2 * core}
    by_x = partner | {"col": core + 2 * (1 - x)}
    by_y = partner | {"grp": 1 - y}

    def along(where):
        return partner | {"row": where}

    barrier = pltpu.get_barrier_semaphore()
    for target in (by_core, by_x, by_y, along(lax.rem(z + 1, 4)), along(lax.rem(z + 2, 4)), along(lax.rem(z + 3, 4))):
        pl.semaphore_signal(barrier, inc=1, device_id=target, device_id_type=MESH)
    pl.semaphore_wait(barrier, 6)

    def remote(slot, source, target_ref, target):
        return pltpu.make_async_remote_copy(
            src_ref=source, dst_ref=target_ref, send_sem=send_sem.at[slot], recv_sem=recv_sem.at[slot],
            device_id=target, device_id_type=MESH,
        )

    def spread(base, source, slots):
        return {
            "in": remote(base, source, slots.at[1], along(near)),
            "out": remote(base + 1, source, slots.at[0], along(outward)),
            "over": remote(base + 2, source, slots.at[0], along(across)),
            "out2": remote(base + 3, slots.at[0], slots.at[1], along(outward)),
            "over2": remote(base + 4, slots.at[1], slots.at[2], along(across)),
            "out3": remote(base + 5, slots.at[2], slots.at[2], along(outward)),
        }

    def fetch_a(index, step, slot):
        columns = pl.ds(pl.multiple_of(index * depth, depth), depth)
        rows = pl.ds(pl.multiple_of(step * tile, tile), tile)
        return pltpu.make_async_copy(a_hbm.at[rows, columns], a_buf.at[slot], a_sem.at[slot])

    def fetch_b(step, slot):
        columns = pl.ds(pl.multiple_of(step * tile, tile), tile)
        return pltpu.make_async_copy(b_hbm.at[:, columns], b_buf.at[slot], b_sem.at[slot])

    def fetch_v(step):
        rows = pl.ds(pl.multiple_of(step * tile, tile), tile)
        return pltpu.make_async_copy(v_hbm.at[rows, :], v_buf.at[rows, :], v_sem.at[step])

    gather_v = spread(0, own_hbm, v_all)
    gather_w = spread(6, w_own, w_all)

    @pl.when(edge)
    def _():
        gather_v["in"].start()

    @pl.when(inside)
    def _():
        gather_v["over"].start()
        gather_v["out"].start()

    fetch_a(dests[0], 0, 0).start()
    fetch_v(0).start()
    for step in range(1, steps):
        fetch_v(step).start()
    fetch_own = pltpu.make_async_copy(own_hbm, own, local_sem.at[0])
    fetch_own.start()

    outer = [remote(12 + i, part.at[i], outer_in.at[i], along(near)) for i in range(3)]
    inner = [remote(15 + i, outer_in.at[i], inner_in.at[i], along(across)) for i in range(2)]
    final = remote(17, inner_in.at[0], final_in, along(outward))
    pass_q = remote(39, q_acc, q_in, along(near))
    fetch_slots = [pltpu.make_async_copy(v_all.at[i], slots.at[i], slot_sem.at[i]) for i in range(3)]

    def product(i):
        def body(step, carry):
            slot = lax.rem(step, 2)
            if i == 0:
                fetch_v(step).wait()
            following = dests[i + 1] if i < 3 else dests[i]
            index = jnp.where(step < steps - 1, dests[i], following)
            ahead = lax.rem(step + 1, steps)
            if i < 3:
                fetch_a(index, ahead, 1 - slot).start()
            else:
                @pl.when(step < steps - 1)
                def _():
                    fetch_a(index, ahead, 1 - slot).start()
            fetch_a(dests[i], step, slot).wait()
            rows = pl.ds(pl.multiple_of(step * tile, tile), tile)
            value = triple(a_buf[slot], v_buf[rows, :], ((0,), (0,)))

            @pl.when(step == 0)
            def _():
                part[i] = value

            @pl.when(step > 0)
            def _():
                part[i] += value

            return carry

        lax.fori_loop(0, steps, body, 0)

    for i in range(3):
        product(i)

        @pl.when(edge)
        def _():
            outer[i].start()

        if i == 1:
            @pl.when(inside)
            def _():
                gather_v["over"].wait_recv()
                gather_v["out2"].start()
                gather_v["in"].wait_recv()
                gather_v["over2"].start()

    @pl.when(inside)
    def _():
        outer[0].wait_recv()
        outer_in[0] += part[0]
        inner[0].start()
        gather_v["over2"].wait_recv()
        gather_v["out3"].start()
        for copy in fetch_slots:
            copy.start()

    fetch_b(0, 0).start()
    product(3)
    fetch_own.wait()
    total[...] = triple(own[...], part[3], ((0,), (0,)))

    def project_b(step, carry):
        slot = lax.rem(step, 2)

        @pl.when(step < steps - 1)
        def _():
            fetch_b(step + 1, 1 - slot).start()

        fetch_b(step, slot).wait()
        rows = pl.ds(pl.multiple_of(step * tile, tile), tile)
        value = triple(b_buf[slot], v_buf[rows, :], ((1,), (0,)))

        @pl.when(step == 0)
        def _():
            q_acc[...] = value

        @pl.when(step > 0)
        def _():
            q_acc[...] += value

        return carry

    lax.fori_loop(0, steps // 2, project_b, 0)

    @pl.when(inside)
    def _():
        outer[1].wait_recv()
        outer_in[1] += part[1]
        inner[1].start()
        inner[0].wait_recv()
        inner_in[0] += part[2]
        final.start()

    @pl.when(edge)
    def _():
        for name in ("out", "out2", "out3"):
            gather_v[name].wait_recv()
        for copy in fetch_slots:
            copy.start()

    for copy in fetch_slots:
        copy.wait()
    total[...] += triple(slots[2], part[0], ((0,), (0,)))
    total[...] += triple(slots[jnp.where(edge, 0, 1)], part[2], ((0,), (0,)))
    total[...] += triple(slots[jnp.where(edge, 1, 0)], part[1], ((0,), (0,)))

    def piece(start, size):
        return pl.ds(pl.multiple_of(start, size), size)

    sizes = [depth // 2, depth // 4, depth // 8]
    bits, targets, landings = [core, x, y], [by_core, by_x, by_y], [half_in, quarter_in, eighth_in]
    base = 0
    reduces = []
    for i in range(3):
        other = base + (1 - bits[i]) * sizes[i]
        base = base + bits[i] * sizes[i]
        copy = remote(31 + i, total.at[piece(other, sizes[i])], landings[i], targets[i])
        copy.start()
        if i == 0:
            lax.fori_loop(steps // 2, steps, project_b, 0)
        copy.wait_recv()
        here = piece(base, sizes[i])
        total[here, :] += landings[i][...]
        reduces.append(copy)
    mine = piece(base, sizes[2])
    line = [
        remote(34, total.at[mine], line_in, along(beside)),
        remote(35, eighth_in, far_in, along(lax.rem(z + 2, 4))),
    ]
    line[0].start()

    @pl.when(inside)
    def _():
        inner[1].wait_recv()
        part[3] += inner_in[1]
        outer[2].wait_recv()
        part[3] += outer_in[2]

    @pl.when(edge)
    def _():
        final.wait_recv()
        part[3] += final_in[...]

    w_own[...] = triple(part[3], t_ref[...], ((1,), (0,)))

    half = depth // 2
    places = [pl.ds(i * depth, half) for i in range(8)], [pl.ds(i * depth + half, half) for i in range(8)]
    top, bottom = pl.ds(0, half), pl.ds(half, half)
    hops = [
        remote(18, w_own.at[top], w_rows.at[places[0][1]], by_y),
        remote(19, w_own.at[bottom], w_rows.at[places[1][2]], by_x),
        remote(20, w_own.at[top], w_rows.at[places[0][2]], by_x),
        remote(21, w_own.at[bottom], w_rows.at[places[1][1]], by_y),
        remote(22, w_rows.at[places[0][1]], w_rows.at[places[0][3]], by_x),
        remote(23, w_rows.at[places[1][2]], w_rows.at[places[1][3]], by_y),
    ]
    shares = [remote(24, w_own, w_rows.at[pl.ds(4 * depth, depth)], by_core)]
    for slot, (side, i) in enumerate([(0, 1), (1, 2), (0, 2), (1, 1), (0, 3), (1, 3)]):
        shares.append(remote(25 + slot, w_rows.at[places[side][i]], w_rows.at[places[side][4 + i]], by_core))

    for hop in hops[:3]:
        hop.start()
    shares[0].start()
    put_w = pltpu.make_async_copy(w_own, w_rows.at[pl.ds(0, depth)], local_sem.at[2])
    put_w.start()

    line[0].wait()
    eighth_in[...] = total[mine, :] + line_in[...]
    line[1].start()

    @pl.when(edge)
    def _():
        gather_w["in"].start()
        pass_q.start()

    @pl.when(inside)
    def _():
        gather_w["over"].start()
        gather_w["out"].start()

    line[1].wait()
    cross[mine, :] = eighth_in[...] + far_in[...]
    returns = []
    for i in (2, 1, 0):
        here = piece(base - lax.rem(base, sizes[i]), sizes[i])
        returns.append(remote(36 + i, cross.at[here], cross.at[here], targets[i]))
    returns[0].start()
    hops[3].start()
    returns[0].wait_recv()
    returns[1].start()
    for i in range(2):
        hops[i].wait_recv()
        hops[4 + i].start()
        shares[1 + i].start()
    returns[1].wait_recv()
    returns[2].start()

    @pl.when(inside)
    def _():
        gather_w["over"].wait_recv()
        gather_w["out2"].start()
        gather_w["in"].wait_recv()
        gather_w["over2"].start()

    for i in range(2, 4):
        hops[i].wait_recv()
        shares[1 + i].start()
    returns[2].wait()
    far_product = triple(cross[...], t_ref[...], ((1,), (0,)))
    own[...] = triple(t_ref[...], far_product, ((0,), (0,)))
    put_y = pltpu.make_async_copy(own, y_out, local_sem.at[3])
    put_y.start()
    for i in range(4, 6):
        hops[i].wait_recv()
        shares[1 + i].start()

    @pl.when(inside)
    def _():
        pass_q.wait_recv()
        q_acc[...] += q_in[...]

    put_q = pltpu.make_async_copy(q_acc, q_out, local_sem.at[1])

    @pl.when(edge)
    def _():
        pass_q.wait_send()

    put_q.start()
    for copy in hops + shares + reduces + returns[:2]:
        copy.wait_send()
    for copy in shares:
        copy.wait_recv()
    put_w.wait()
    put_q.wait()
    put_y.wait()

    @pl.when(edge)
    def _():
        gather_v["in"].wait_send()
        gather_w["in"].wait_send()
        for copy in outer:
            copy.wait_send()
        for name in ("out", "out2"):
            gather_w[name].wait_recv()

    @pl.when(inside)
    def _():
        for name in ("over", "out", "out2", "over2", "out3"):
            gather_v[name].wait_send()
        for name in ("over", "out", "out2", "over2"):
            gather_w[name].wait_send()
        for copy in inner + [final]:
            copy.wait_send()
        gather_w["over2"].wait_recv()


def front(matrix, reflectors, own_v, basis_rows, tfactor):
    depth, wide = own_v.shape
    rows = reflectors.shape[0]
    tile = rows // 4
    hbm = pl.BlockSpec(memory_space=pltpu.HBM)
    chunk = (depth, wide)

    def shape(*dims):
        return jax.ShapeDtypeStruct(dims, jnp.float32)

    def vmem(*dims):
        return pltpu.VMEM(dims, jnp.float32)

    return pl.pallas_call(
        front_kernel,
        out_shape=[shape(3, *chunk), shape(3, *chunk), shape(8 * depth, wide), shape(*chunk), shape(*chunk)],
        in_specs=[hbm] * 4 + [pl.BlockSpec(memory_space=pltpu.VMEM)],
        out_specs=[hbm] * 5,
        scratch_shapes=[
            vmem(2, tile, depth), vmem(2, depth, tile), vmem(rows, wide), vmem(*chunk), vmem(4, *chunk),
            vmem(3, *chunk), vmem(2, *chunk), vmem(*chunk), vmem(*chunk), vmem(*chunk), vmem(*chunk),
            vmem(*chunk), vmem(*chunk), vmem(3, *chunk),
            vmem(depth // 2, wide), vmem(depth // 4, wide), vmem(depth // 8, wide), vmem(depth // 8, wide),
            vmem(depth // 8, wide),
            pltpu.SemaphoreType.DMA((2,)), pltpu.SemaphoreType.DMA((2,)), pltpu.SemaphoreType.DMA((4,)),
            pltpu.SemaphoreType.DMA((3,)), pltpu.SemaphoreType.DMA((4,)), pltpu.SemaphoreType.DMA((40,)),
            pltpu.SemaphoreType.DMA((40,)),
        ],
        compiler_params=pltpu.CompilerParams(
            collective_id=0, has_side_effects=True, vmem_limit_bytes=60 * 1024 * 1024
        ),
        cost_estimate=pl.CostEstimate(
            flops=30 * rows * depth * wide, bytes_accessed=20 * rows * depth, transcendentals=0
        ),
        name="front",
    )(matrix, reflectors, own_v, basis_rows, tfactor)


def finish_kernel(wide_calls, order_ref, a_ref, w_ref, v_ref, y_ref, *rest):
    (*chunks, out_ref, left, right), count = rest, wide_calls
    first = (pl.program_id(0) == 0) & (pl.program_id(1) == 0)

    @pl.when(first)
    def _():
        for i in range(count):
            v_chunk = chunks[2 * i][...]
            w_chunk = chunks[2 * i + 1][...]
            if len(chunks) % 2 == 1 and count == 1:
                w_chunk = jnp.where(order_ref[1] > 0, chunks[2][...], w_chunk)
            z_high, z_low = halves(w_chunk - triple(v_chunk, y_ref[...], ((1,), (1,))))
            v_high, v_low = halves(v_chunk)
            right[i] = jnp.concatenate([v_high, v_high, v_low, z_high, z_high, z_low], axis=1)

    @pl.when(pl.program_id(1) == 0)
    def _():
        w_high, w_low = halves(w_ref[...])
        v_high, v_low = halves(v_ref[...])
        left[...] = jnp.concatenate([w_high, w_low, w_high, v_high, v_low, v_high], axis=1)

    out_ref[...] = a_ref[...] - lax.dot_general(
        left[...], right[pl.program_id(1)], (((1,), (1,)), ((), ())), preferred_element_type=jnp.float32
    )


def finish(matrix, w_rows, v_row, inner, owners, flag, tiles, chunks, out):
    rows, wide = v_row.shape
    depth = inner.shape[0]
    count, steps = owners.shape[0], tiles.shape[0]
    tile, lead = rows // steps, count + 1
    order = jnp.concatenate([owners, flag, tiles]).astype(jnp.int32)
    specs = [
        pl.BlockSpec((tile, depth), lambda i, j, c: (c[i + lead], c[j])),
        pl.BlockSpec((tile, wide), lambda i, j, c: (i, 0)),
        pl.BlockSpec((tile, wide), lambda i, j, c: (c[i + lead], 0)),
        pl.BlockSpec(inner.shape, lambda i, j, c: (0, 0)),
    ]
    args = [matrix, w_rows, v_row, inner]
    for array, slot in chunks:
        if array.ndim == 3:
            specs.append(pl.BlockSpec((None, depth, wide), lambda i, j, c, at=slot: (at, 0, 0)))
        else:
            specs.append(pl.BlockSpec((depth, wide), lambda i, j, c, at=slot: (at, 0)))
        args.append(array)
    kernel, alias = functools.partial(finish_kernel, count), {}
    if out is not None:
        specs.append(pl.BlockSpec(memory_space=pl.ANY))
        args.append(out)
        alias = {len(args): 0}
        inside = kernel

        def kernel(*refs):
            inside(*refs[: len(args)], *refs[len(args) + 1 :])

    return pl.pallas_call(
        kernel,
        out_shape=jax.ShapeDtypeStruct(matrix.shape, jnp.float32),
        grid_spec=pltpu.PrefetchScalarGridSpec(
            num_scalar_prefetch=1,
            grid=(steps, count),
            in_specs=specs,
            out_specs=pl.BlockSpec((tile, depth), lambda i, j, c: (c[i + lead], c[j])),
            scratch_shapes=[
                pltpu.VMEM((tile, 6 * wide), jnp.bfloat16),
                pltpu.VMEM((count, depth, 6 * wide), jnp.bfloat16),
            ],
        ),
        input_output_aliases=alias,
        cost_estimate=pl.CostEstimate(
            flops=12 * rows * depth * wide * count,
            bytes_accessed=8 * rows * (depth * count + wide),
            transcendentals=0,
        ),
        name="finish",
    )(order, *args)


def send(x, pairs):
    return lax.ppermute(x, "row", pairs)


def line_step(matrix, basis_rows, reflectors, tfactor):
    z, col, y = (lax.axis_index(name) for name in ("row", "col", "grp"))
    member, groups = lax.axis_index(("col", "grp")), lax.axis_size(("col", "grp"))
    depth = reflectors.shape[0] // groups
    own_v = lax.dynamic_slice_in_dim(reflectors, member * depth, depth, 0)
    v_all, w_all, w_rows, q_pair, inner = front(matrix, reflectors, own_v, basis_rows, tfactor)

    bits = jnp.arange(8)
    tiles = (col ^ (2 * (bits // 2 % 2) + bits // 4)) * 2 + (y ^ (bits % 2))
    edge, low = (z == 0) | (z == 3), z < 2
    owners = jnp.stack([
        z,
        jnp.where(edge, jnp.where(low, 1, 2), jnp.where(low, 2, 1)),
        jnp.where(edge, jnp.where(low, 2, 1), jnp.where(low, 0, 3)),
        jnp.where(low, 3, 0),
    ])
    flag = edge.astype(jnp.int32).reshape(1)
    w_last = send(w_all[2], FINAL)
    q_full = q_pair + send(q_pair, INNER)

    chunks = [(own_v, 0), (w_rows, 0), (v_all, 0), (w_all, 0), (v_all, 1), (w_all, 1)]
    out = finish(matrix, w_rows, reflectors, inner, owners[:3], flag, tiles, chunks, None)
    out, w_last, q_full = lax.optimization_barrier((out, w_last, q_full))
    q_last = send(q_full, FINAL)
    chunks = [(v_all, 2), (w_all, 2), (w_last, 0)]
    out = finish(matrix, w_rows, reflectors, inner, owners[3:], flag, tiles, chunks, out)

    out, q_full, q_last = lax.optimization_barrier((out, q_full, q_last))
    q_full = jnp.where(edge, q_last, q_full)
    new_basis = basis_rows - dot(dot(q_full, tfactor), reflectors.T)
    return (out, new_basis)


def on_device(*args):
    sizes = tuple(lax.axis_size(name) for name in ("row", "col", "grp"))
    return (line_step if sizes == (4, 4, 2) else ring_step)(*args)


def solution(mesh):
    placed = (P("row", ("col", "grp")), P(("col", "grp"), "row"), P("row", None), P())
    return jax.shard_map(
        on_device,
        mesh=mesh,
        in_specs=placed,
        out_specs=(P("row", ("col", "grp")), P(("col", "grp"), "row")),
        check_vma=False,
    )
```
